32 devices in a mesh: sweep: 2 (over x), cell: 8 (over z, y), head: 2 (over core).
Axes of the slice: x: 2, y: 2, z: 4, core: 2. Of those that a mesh axis runs over, the one named last changes fastest.
Arguments:
- hidden: bfloat16 [4096, 8192], P(('sweep', 'cell'), 'head'), parts along dimension 0, may hold values from -6 to 6
- w_key: bfloat16 [8192, 512], P(None, 'head'), may hold values from -0.0625 to 0.0625
- w_value: bfloat16 [8192, 512], P(None, 'head'), may hold values from -0.0625 to 0.0625
- queries: bfloat16 [4096, 4096], P(('sweep', 'cell'), 'head'), parts along dimension 0, as said below
- span_order: int32 [16, 8], P(('sweep', 'cell')), parts along dimension 0, may hold values from 0 to 7, as said below
- span_count: int32 [16], P(('sweep', 'cell')), parts along dimension 0, may hold values from 2 to 8
- needle: int32 [16], P(('sweep', 'cell')), parts along dimension 0, may hold values from 0 to 7, as said below
- owners: int32 [8, 2], P('sweep'), parts along dimension 0, may hold values from 0 to 7, as said below
Outputs:
- attended: bfloat16 [4096, 4096], P(('sweep', 'cell'), 'head'), parts along dimension 0
The draws below stay inside these ranges and needn't reach their ends.
There are 2 independent parts, one for each index of `sweep`. The reference program is written for one: setup_inputs(seed, part) draws one part's arguments, and reference() takes and returns one part's arrays. A program takes and returns all parts, laid end to end along the dimension named above; an argument that names none is the same for every part. Nothing has to cross between parts.
Inputs may be any that keep to these rules, and one draw needn't show every extreme that they name: `span_order`: every row is a permutation of 0 to 7. `needle`: below the same cell's span_count. `owners`: all 8 entries of a part are distinct. `queries`: every entry lies in -64 to 64.
All inputs are finite; a program needn't handle non-finite values.
Results may differ from the reference program's by a relative error of at most 0.004.
The reference program's roundings to bfloat16 on the way count: a program that leaves them out, or rounds other values in their place, can miss the bound.
Values may be sent and summed in bfloat16 or wider, within the bound.
No kernel may reach another device: no remote copies, remote signals or barrier semaphores. Data moves between devices by JAX's collectives and lax.ppermute only.
A program may use at most 128 MiB of HBM per device.

```python
import math
import jax
import jax.numpy as jnp
from jax import lax

D = 8192
HD = 128
KVH = 4
QH = 32
CH = 256
ROUNDS = 4
GROUP = 8
CELLS = 8
SLOTS = 8


def draw_queries(key, part):
    full_shape = (CELLS * CH, QH * HD)
    return jnp.clip(jax.random.normal(key, full_shape, jnp.float32), -6.0, 6.0).astype(jnp.bfloat16)


def cell_plan(key):
    base_key = jax.random.fold_in(key, 11)
    cell_keys = jax.random.split(jax.random.fold_in(base_key, 1), CELLS)
    cell_order = jax.vmap(lambda sub_key: jax.random.permutation(sub_key, SLOTS))(cell_keys).astype(jnp.int32)
    cell_ids = jnp.arange(CELLS, dtype=jnp.int32)
    full_cell = jax.random.randint(jax.random.fold_in(base_key, 2), (), 0, CELLS)
    short_cell = (full_cell + 1) % CELLS
    cell_count = jax.random.randint(jax.random.fold_in(base_key, 3), (CELLS,), 2, SLOTS + 1)
    cell_count = jnp.where(cell_ids == full_cell, SLOTS, jnp.where(cell_ids == short_cell, 2, cell_count)).astype(jnp.int32)
    needle_slot = jax.random.randint(jax.random.fold_in(base_key, 4), (CELLS,), 0, cell_count)
    needle_slot = jnp.where(cell_ids == full_cell, SLOTS - 1, needle_slot).astype(jnp.int32)
    return (cell_order, cell_count, needle_slot)


def draw_span_order(key, part):
    return cell_plan(key)[0]


def draw_span_count(key, part):
    return cell_plan(key)[1]


def draw_needle(key, part):
    return cell_plan(key)[2]


def draw_owners(key, part):
    shuffled = jax.random.permutation(jax.random.fold_in(key, 5), CELLS).astype(jnp.int32)
    target = jnp.argmax(shuffled == CELLS - 1)
    place = jax.random.randint(jax.random.fold_in(key, 6), (), 0, min(SLOTS, CELLS))
    moved = shuffled[place]
    shuffled = shuffled.at[target].set(moved).at[place].set(CELLS - 1)
    return shuffled[jnp.arange(SLOTS) % CELLS].reshape(ROUNDS, 2).astype(jnp.int32)


def steps_of(stream_key, dims, cuts, least, top_value):
    factor_of, own = 1.0, jax.random.fold_in(stream_key, 6)
    for axis_at, blocks in cuts:
        draws = jnp.exp(jax.random.uniform(jax.random.fold_in(own, axis_at), (blocks,), jnp.float32, least / len(cuts), top_value / len(cuts)))
        factor_of = factor_of * jnp.repeat(draws, dims[axis_at] // blocks).reshape([-1 if axis == axis_at else 1 for axis in range(len(dims))])
    return factor_of


def scatter_about(rng, extent, scale, bound, pieces=(), kind=jnp.bfloat16):
    result = jax.random.normal(rng, extent, jnp.float32) * scale
    if len(pieces) > 0:
        result = steps_of(rng, extent, pieces, -0.22, 0.18) * result
    return jnp.clip(result, min=-bound, max=bound).astype(kind)


def setup_inputs(seed: int = 0, part: int = 0) -> dict:
    key_list = jax.random.split(jax.random.key(seed), 9)
    part_splits = jax.random.split(jax.random.fold_in(key_list[8], part), 9)
    hidden = scatter_about(part_splits[0], (CELLS * CH, D), 1.0, 6.0, ((0, 8), (1, 2)))
    w_key = scatter_about(key_list[1], (D, KVH * HD), D ** -0.5, 0.0625, ((1, 2),))
    w_value = scatter_about(key_list[2], (D, KVH * HD), D ** -0.5, 0.0625, ((1, 2),))
    queries = draw_queries(jax.random.fold_in(jax.random.fold_in(key_list[8], part), 71), part)
    span_order = draw_span_order(jax.random.fold_in(jax.random.fold_in(key_list[8], part), 71), part)
    span_count = draw_span_count(jax.random.fold_in(jax.random.fold_in(key_list[8], part), 71), part)
    needle = draw_needle(jax.random.fold_in(jax.random.fold_in(key_list[8], part), 71), part)
    owners = draw_owners(jax.random.fold_in(jax.random.fold_in(key_list[8], part), 71), part)
    return dict(hidden=hidden, w_key=w_key, w_value=w_value, queries=queries, span_order=span_order, span_count=span_count, needle=needle, owners=owners)


rope_theta = 500000.0

def rotary(values, positions):
    half_dim = values.shape[-1] // 2
    frequency = rope_theta ** (-2.0 * jnp.arange(half_dim, dtype=jnp.float32) / values.shape[-1])
    angles = positions.astype(jnp.float32)[..., None] * frequency
    cosine = jnp.cos(angles)
    sine_part = jnp.sin(angles)
    first = values[..., :half_dim]
    second = values[..., half_dim:]
    return jnp.concatenate([first * cosine - second * sine_part, second * cosine + first * sine_part], axis=-1)

def reference(hidden, w_key, w_value, queries, span_order, span_count, needle, owners):
    key_rows = jnp.dot(hidden, w_key, preferred_element_type=jnp.float32).astype(jnp.bfloat16)
    value_rows = jnp.dot(hidden, w_value, preferred_element_type=jnp.float32).astype(jnp.bfloat16)
    slot_owner = owners.reshape(-1)
    slot_total = slot_owner.shape[0]
    context_keys = key_rows.reshape(CELLS, CH, KVH, HD)[slot_owner].astype(jnp.float32)
    context_values = value_rows.reshape(CELLS, CH, KVH, HD)[slot_owner].reshape(slot_total * CH, KVH, HD).astype(jnp.float32)
    lane_ids = jnp.arange(CH, dtype=jnp.int32)
    slot_ids = jnp.arange(slot_total, dtype=jnp.int32)
    score_scale = 1.0 / math.sqrt(HD)

    def one_cell(cell_item):
        query_rows, cell_order, cell_count, needle_slot = cell_item
        key_pos = cell_order[:, None] * CH + lane_ids[None, :]
        rot_keys = rotary(context_keys, key_pos[:, :, None]).astype(jnp.bfloat16)
        rot_keys = lax.optimization_barrier(rot_keys).astype(jnp.float32).reshape(slot_total * CH, KVH, HD)
        query_pos = cell_order[needle_slot] * CH + lane_ids
        rot_query = rotary(query_rows.reshape(CH, KVH, GROUP, HD).astype(jnp.float32), query_pos[:, None, None]).astype(jnp.bfloat16)
        rot_query = lax.optimization_barrier(rot_query).astype(jnp.float32)
        scores = jnp.einsum('ikgd,jkd->ikgj', rot_query, rot_keys) * score_scale
        before = (slot_ids < cell_count) & (cell_order < cell_order[needle_slot])
        causal = (slot_ids == needle_slot)[:, None, None] & (lane_ids[None, None, :] <= lane_ids[None, :, None])
        visible = jnp.transpose(before[:, None, None] | causal, (1, 0, 2)).reshape(CH, slot_total * CH)
        scores = jnp.where(visible[:, None, None, :], scores, -jnp.inf)
        running_max = lax.optimization_barrier(jnp.max(scores, axis=-1, keepdims=True))
        weights = jnp.exp(scores - running_max)
        weight_sum = lax.optimization_barrier(jnp.sum(weights, axis=-1))
        rounded = lax.optimization_barrier(weights.astype(jnp.bfloat16)).astype(jnp.float32)
        mixed_rows = jnp.einsum('ikgj,jkd->ikgd', rounded, context_values)
        return (mixed_rows / weight_sum[..., None]).astype(jnp.bfloat16).reshape(CH, QH * HD)
    outputs = lax.map(one_cell, (queries.reshape(CELLS, CH, QH * HD), span_order, span_count, needle))
    return outputs.reshape(CELLS * CH, QH * HD)
```

```python
import functools
import math

import jax
import jax.numpy as jnp
import numpy as np
from jax import lax
from jax.experimental import pallas as pl
from jax.experimental.pallas import tpu as pltpu
from jax.sharding import PartitionSpec as P

HD = 128
GROUP = 8
ROPE_THETA = 500000.0
NEG = -1e30
RING_LIMIT = 16
VMEM_LIMIT = 24 * 1024 * 1024


def rotary_tables(rows, slots):
    half = HD // 2
    frequency = ROPE_THETA ** (-2.0 * np.arange(half, dtype=np.float64) / HD)

    def pair(positions):
        angle = positions[:, None] * frequency[None, :]
        cosine, sine = np.cos(angle), np.sin(angle)
        return (
            np.concatenate([cosine, cosine], axis=1),
            np.concatenate([-sine, sine], axis=1),
        )

    row = np.stack(pair(np.arange(rows, dtype=np.float64)))
    place = np.stack(pair(rows * np.arange(slots, dtype=np.float64)), axis=1)
    return row.astype(np.float32), place.astype(np.float32)


def table_at(row_ref, place_ref, place):
    rc, rs = row_ref[0], row_ref[1]
    at = place_ref[place]
    pc, ps = at[0:1], at[1:2]
    return rc * pc - rs * ps, rs * pc + rc * ps


def rotate(values, cosine, sine):
    x = values.astype(jnp.float32)
    return (x * cosine + pltpu.roll(x, HD // 2, 1) * sine).astype(jnp.bfloat16)


def project_body(first, last, rotate_heads, meta, hid, wk, wv, *rest):
    step = pl.program_id(0)
    rest = list(rest)
    part = None if first else rest.pop(0)
    if rotate_heads:
        q, row_t, place_t = rest[:3]
        rest = rest[3:]
    out = rest.pop(0)
    if rotate_heads:
        q_out = rest.pop(0)
    acc = rest.pop(0)
    width = wk.shape[1]

    @pl.when(step == 0)
    def _():
        if first:
            acc[...] = jnp.zeros_like(acc)
        else:
            acc[...] = part[...]

    x = hid[...]
    acc[:, :width] += jnp.dot(x, wk[...], preferred_element_type=jnp.float32)
    acc[:, width:] += jnp.dot(x, wv[...], preferred_element_type=jnp.float32)
    if rotate_heads:
        place = meta[4 + meta[3]]
        cosine, sine = table_at(row_t, place_t, place)
        for h in range(q.shape[1] // HD):
            q_out[h] = rotate(q[:, h * HD : (h + 1) * HD], cosine, sine)

    @pl.when(step == pl.num_programs(0) - 1)
    def _():
        if last:
            out[0] = acc[:, :width].astype(jnp.bfloat16)
            out[1] = acc[:, width:].astype(jnp.bfloat16)
        else:
            out[...] = acc[...]


def project(shift, heads, meta, hid, wk, wv, part=None, q=None, tables=None, last=False):
    rows, depth = hid.shape
    width = wk.shape[1]
    tiles = 4
    tk = depth // tiles
    first = part is None

    def w_map(k, meta):
        return (lax.rem(meta[0] + shift, heads) * tiles + k, 0)

    in_specs = [
        pl.BlockSpec((rows, tk), lambda k, meta: (0, k)),
        pl.BlockSpec((tk, width), w_map),
        pl.BlockSpec((tk, width), w_map),
    ]
    operands = [hid, wk, wv]
    if not first:
        in_specs.append(pl.BlockSpec((rows, 2 * width), lambda k, meta: (0, 0)))
        operands.append(part)
    if last:
        out_shape = [jax.ShapeDtypeStruct((2, rows, width), jnp.bfloat16)]
        out_specs = [pl.BlockSpec((2, rows, width), lambda k, meta: (0, 0, 0))]
    else:
        out_shape = [jax.ShapeDtypeStruct((rows, 2 * width), jnp.float32)]
        out_specs = [pl.BlockSpec((rows, 2 * width), lambda k, meta: (0, 0))]
    if q is not None:
        row_t, place_t = tables
        q_heads = q.shape[1] // HD
        per = q_heads // tiles
        in_specs += [
            pl.BlockSpec((rows, per * HD), lambda k, meta: (0, k)),
            pl.BlockSpec(row_t.shape, lambda k, meta: (0, 0, 0)),
            pl.BlockSpec(place_t.shape, lambda k, meta: (0, 0, 0)),
        ]
        operands += [q, row_t, place_t]
        out_shape.append(jax.ShapeDtypeStruct((q_heads, rows, HD), jnp.bfloat16))
        out_specs.append(pl.BlockSpec((per, rows, HD), lambda k, meta: (k, 0, 0)))
    return pl.pallas_call(
        functools.partial(project_body, first, last, q is not None),
        grid_spec=pltpu.PrefetchScalarGridSpec(
            num_scalar_prefetch=1,
            grid=(tiles,),
            in_specs=in_specs,
            out_specs=out_specs,
            scratch_shapes=[pltpu.VMEM((rows, 2 * width), jnp.float32)],
        ),
        out_shape=out_shape,
        compiler_params=pltpu.CompilerParams(vmem_limit_bytes=VMEM_LIMIT),
        name="project",
    )(meta, *operands)


def attend_body(cells, offsets, ring, first, last, meta, q, row_t, place_t, *rest):
    rest = list(rest)
    blocks = [rest.pop(0) for _ in (offsets if ring else (0,))]
    if not first:
        m_in, l_in, acc_in = rest[:3]
        rest = rest[3:]
    if last:
        out, m, l, acc, k_rot = rest
    else:
        m, l, acc, k_rot = rest
    rows = q.shape[1]
    slots = place_t.shape[0]
    coef = math.log2(math.e) / math.sqrt(HD)
    count, needle = meta[2], meta[3]
    needle_place = meta[4 + needle]
    group = q.shape[0]

    if first:
        m[...] = jnp.full_like(m, NEG)
        l[...] = jnp.zeros_like(l)
        acc[...] = jnp.zeros_like(acc)
    else:
        m[...] = m_in[...]
        l[...] = l_in[...]
        acc[...] = acc_in[...]

    def head_step(h, values, causal):
        s = lax.dot_general(
            q[h], k_rot[...], (((1,), (1,)), ((), ())), preferred_element_type=jnp.float32
        )
        if causal:
            row = lax.broadcasted_iota(jnp.int32, s.shape, 0)
            col = lax.broadcasted_iota(jnp.int32, s.shape, 1)
            s = jnp.where(col <= row, s, -jnp.inf)
        m_old = m[h]
        m_new = jnp.maximum(m_old, jnp.max(s, axis=1, keepdims=True))
        m[h] = m_new
        p = jnp.exp2((s - m_new[:, 0:1]) * coef)
        alpha = jnp.exp2((m_old - m_new) * coef)
        l[h] = l[h] * alpha + jnp.sum(p, axis=1, keepdims=True)
        acc[h] = acc[h] * alpha + jnp.dot(
            p.astype(jnp.bfloat16), values, preferred_element_type=jnp.float32
        )

    def span_step(k_block, v_block, slot):
        place = meta[4 + slot]
        cosine, sine = table_at(row_t, place_t, place)
        k_rot[...] = rotate(k_block, cosine, sine)
        before = (slot < count) & (place < needle_place)

        @pl.when(before)
        def _():
            for h in range(group):
                head_step(h, v_block, False)

        @pl.when(slot == needle)
        def _():
            for h in range(group):
                head_step(h, v_block, True)

    def owner_slot(cell):
        found = jnp.int32(-1)
        for s in range(slots):
            found = jnp.where(meta[4 + slots + s] == cell, s, found)
        return found

    if ring:
        for offset, block in zip(offsets, blocks):
            at = lax.rem(meta[1] + offset + cells, cells)
            evens = (cells + 1) // 2
            cell = jnp.where(at < evens, 2 * at, 2 * (cells - at) - 1)
            slot = owner_slot(cell)
            place = meta[4 + jnp.maximum(slot, 0)]
            seen = (slot >= 0) & (
                ((slot < count) & (place < needle_place)) | (slot == needle)
            )

            @pl.when(seen)
            def _():
                span_step(block[0], block[1], slot)
    else:
        def loop(slot, carry):
            place = meta[4 + slot]

            @pl.when(((slot < count) & (place < needle_place)) | (slot == needle))
            def _():
                cell = meta[4 + slots + slot]
                span_step(blocks[0][cell, 0], blocks[0][cell, 1], slot)

            return carry

        lax.fori_loop(0, slots, loop, 0)

    if last:
        for h in range(group):
            out[:, h * HD : (h + 1) * HD] = (acc[h] / l[h]).astype(jnp.bfloat16)


def attend(cells, offsets, ring, meta, q, tables, blocks, state, last):
    row_t, place_t = tables
    q_heads, rows, _ = q.shape
    kv_heads = q_heads // GROUP
    first = state is None
    head_block = pl.BlockSpec((GROUP, rows, HD), lambda k, meta: (k, 0, 0))
    in_specs = [
        head_block,
        pl.BlockSpec(row_t.shape, lambda k, meta: (0, 0, 0)),
        pl.BlockSpec(place_t.shape, lambda k, meta: (0, 0, 0)),
    ]
    operands = [q, row_t, place_t]
    for block in blocks:
        if block.ndim == 3:
            in_specs.append(pl.BlockSpec((2, rows, HD), lambda k, meta: (0, 0, k)))
        else:
            in_specs.append(
                pl.BlockSpec((block.shape[0], 2, rows, HD), lambda k, meta: (0, 0, 0, k))
            )
        operands.append(block)
    if not first:
        in_specs += [head_block] * 3
        operands += list(state)
    state_shape = jax.ShapeDtypeStruct((q_heads, rows, HD), jnp.float32)
    scratch = [pltpu.VMEM((rows, HD), jnp.bfloat16)]
    if last:
        out_shape = jax.ShapeDtypeStruct((rows, q_heads * HD), jnp.bfloat16)
        out_specs = pl.BlockSpec((rows, GROUP * HD), lambda k, meta: (0, k))
        scratch = [pltpu.VMEM((GROUP, rows, HD), jnp.float32)] * 3 + scratch
    else:
        out_shape = [state_shape] * 3
        out_specs = [head_block] * 3
    return pl.pallas_call(
        functools.partial(attend_body, cells, tuple(offsets), ring, first, last),
        grid_spec=pltpu.PrefetchScalarGridSpec(
            num_scalar_prefetch=1,
            grid=(kv_heads,),
            in_specs=in_specs,
            out_specs=out_specs,
            scratch_shapes=scratch,
        ),
        out_shape=out_shape,
        compiler_params=pltpu.CompilerParams(vmem_limit_bytes=VMEM_LIMIT),
        name="attend",
    )(meta, *operands)


def on_device(cells, heads, hidden, w_key, w_value, queries, span_order, span_count, needle, owners):
    rows = hidden.shape[0]
    slots = span_order.shape[1]
    row_np, place_np = rotary_tables(rows, slots)
    tables = (jnp.asarray(row_np), jnp.asarray(place_np))
    cell = lax.axis_index("cell").astype(jnp.int32)
    ring_place = jnp.where(cell % 2 == 0, cell // 2, cells - (cell + 1) // 2)
    head = lax.axis_index("head").astype(jnp.int32)
    meta = jnp.concatenate(
        [head[None], ring_place[None], span_count, needle, span_order[0], owners.reshape(-1)]
    )

    others = [
        lax.ppermute(hidden, "head", [((h + shift) % heads, h) for h in range(heads)])
        for shift in range(1, heads)
    ]
    part, q = project(0, heads, meta, hidden, w_key, w_value, q=queries, tables=tables)
    for shift, other in enumerate(others, 1):
        (part,) = project(
            shift, heads, meta, other, w_key, w_value, part=part, last=shift == heads - 1
        )
    own = part

    if cells > RING_LIMIT:
        every = lax.all_gather(own, "cell", axis=0)
        return attend(cells, (), False, meta, q, tables, [every], None, True)

    ring = list(range(0, cells, 2)) + list(range(1, cells, 2))[::-1]
    up = [(ring[i], ring[(i + 1) % cells]) for i in range(cells)]
    down = [(b, a) for a, b in up]
    rising, falling = own, own
    state = None
    ready, offsets = [own], [0]
    for step in range(1, cells // 2 + 1):
        rising = lax.ppermute(rising, "cell", up)
        arrived, arrived_at = [rising], [-step]
        if step < cells - step:
            falling = lax.ppermute(falling, "cell", down)
            arrived.append(falling)
            arrived_at.append(step)
        state = attend(cells, offsets, True, meta, q, tables, ready, state, False)
        ready, offsets = arrived, arrived_at
    return attend(cells, offsets, True, meta, q, tables, ready, state, True)


def solution(mesh):
    cells, heads = mesh.shape["cell"], mesh.shape["head"]
    in_specs = (
        P(("sweep", "cell"), "head"),
        P(None, "head"),
        P(None, "head"),
        P(("sweep", "cell"), "head"),
        P(("sweep", "cell"), None),
        P(("sweep", "cell")),
        P(("sweep", "cell")),
        P("sweep", None),
    )
    return jax.shard_map(
        functools.partial(on_device, cells, heads),
        mesh=mesh,
        in_specs=in_specs,
        out_specs=P(("sweep", "cell"), "head"),
        check_vma=False,
    )
```

```python
import functools
import math

import jax
import jax.numpy as jnp
import numpy as np
from jax import lax
from jax.experimental import pallas as pl
from jax.experimental.pallas import tpu as pltpu
from jax.sharding import PartitionSpec as P


HD = 128
GROUP = 8
ROPE_THETA = 500000.0
NEG = -1e30
COEF = math.log2(math.e) / math.sqrt(HD)
SAFE_LOW, SAFE_HIGH = 2.0**-60, 2.0**60
PIPE = 4
RING_LIMIT = 16
VMEM_LIMIT = 24 * 1024 * 1024


def rotary_tables(rows, slots):
    half = HD // 2
    frequency = ROPE_THETA ** (-2.0 * np.arange(half, dtype=np.float64) / HD)

    def pair(positions):
        angle = positions[:, None] * frequency[None, :]
        cosine, sine = np.cos(angle), np.sin(angle)
        return (
            np.concatenate([cosine, cosine], axis=1),
            np.concatenate([-sine, sine], axis=1),
        )

    row = np.stack(pair(np.arange(rows, dtype=np.float64)))
    place = np.stack(pair(rows * np.arange(slots, dtype=np.float64)), axis=1)
    return row.astype(np.float32), place.astype(np.float32)


def table_at(row_ref, place_ref, place):
    rc, rs = row_ref[0], row_ref[1]
    at = place_ref[place]
    pc, ps = at[0:1], at[1:2]
    return rc * pc - rs * ps, rs * pc + rc * ps


def rotate(values, cosine, sine):
    x = values.astype(jnp.float32)
    return (x * cosine + pltpu.roll(x, HD // 2, 1) * sine).astype(jnp.bfloat16)


def find_slot(owners, cell):
    rounds = owners.shape[1]
    found = jnp.int32(-1)
    for r in range(rounds):
        for t in range(owners.shape[0]):
            found = jnp.where(owners[t, r] == cell, r * owners.shape[0] + t, found)
    return found


def prepare_body(heads, order, count, needle, owners, hid, wk, wv, q, row_t, place_t,
                 part, q_t, wk_next, wv_next, order_s, count_s, needle_s, owners_s,
                 hid_buf, wk_buf, wv_buf, q_buf, row_buf, place_buf, sems, small_sems):
    _, depth = hid.shape
    tiles = hid_buf.shape[0]
    tk = depth // tiles
    head = lax.axis_index("head")
    small = [
        pltpu.make_async_copy(source, target, small_sems.at[i])
        for i, (source, target) in enumerate(
            [
                (order, order_s),
                (count, count_s),
                (needle, needle_s),
                (owners, owners_s),
                (row_t, row_buf),
                (place_t, place_buf),
                (q, q_buf),
            ]
        )
    ]
    for copy in small:
        copy.start()
    copies = []
    for t in range(tiles):
        base = pl.multiple_of(head * depth + t * tk, tk)
        trio = (
            pltpu.make_async_copy(hid.at[:, t * tk : (t + 1) * tk], hid_buf.at[t], sems.at[0, t]),
            pltpu.make_async_copy(wk.at[pl.ds(base, tk), :], wk_buf.at[t], sems.at[1, t]),
            pltpu.make_async_copy(wv.at[pl.ds(base, tk), :], wv_buf.at[t], sems.at[2, t]),
        )
        for copy in trio:
            copy.start()
        copies.append(trio)
    other = pl.multiple_of(lax.rem(head + 1, heads) * depth, depth)
    later = [
        pltpu.make_async_copy(wk.at[pl.ds(other, depth), :], wk_next, small_sems.at[7]),
        pltpu.make_async_copy(wv.at[pl.ds(other, depth), :], wv_next, small_sems.at[8]),
    ]
    for copy in later:
        copy.start()
    for copy in small:
        copy.wait()
    cosine, sine = table_at(row_buf, place_buf, order_s[0, needle_s[0]])
    q_heads = q_t.shape[0]
    per = q_heads // tiles
    for t, trio in enumerate(copies):
        for h in range(t * per, (t + 1) * per):
            q_t[h] = rotate(q_buf[:, h * HD : (h + 1) * HD], cosine, sine).T
        for copy in trio:
            copy.wait()
        x = hid_buf[t]
        for side, w in enumerate((wk_buf, wv_buf)):
            product = jnp.dot(x, w[t], preferred_element_type=jnp.float32)
            if t == 0:
                part[side] = product
            else:
                part[side] += product
    for copy in later:
        copy.wait()


def prepare(heads, scalars, hid, wk, wv, q, tables):
    rows, depth = hid.shape
    width = wk.shape[1]
    tiles = 4
    tk = depth // tiles
    operands = [
        pltpu.with_memory_space_constraint(x, pltpu.HBM) if x.size > 1 else x
        for x in (*scalars, hid, wk, wv, q, *tables)
    ]
    hbm = pl.BlockSpec(memory_space=pltpu.HBM)
    vmem = pl.BlockSpec(memory_space=pltpu.VMEM)
    bf16 = jnp.bfloat16
    return pl.pallas_call(
        functools.partial(prepare_body, heads),
        in_specs=[hbm] * len(operands),
        out_specs=[vmem] * 4 + [pl.BlockSpec(memory_space=pltpu.SMEM)] * len(scalars),
        out_shape=[
            jax.ShapeDtypeStruct((2, rows, width), jnp.float32),
            jax.ShapeDtypeStruct((q.shape[1] // HD, HD, rows), bf16),
            jax.ShapeDtypeStruct((depth, width), bf16),
            jax.ShapeDtypeStruct((depth, width), bf16),
            *[jax.ShapeDtypeStruct(x.shape, jnp.int32) for x in scalars],
        ],
        scratch_shapes=[
            pltpu.VMEM((tiles, rows, tk), bf16),
            pltpu.VMEM((tiles, tk, width), bf16),
            pltpu.VMEM((tiles, tk, width), bf16),
            pltpu.VMEM(q.shape, bf16),
            *[pltpu.VMEM(table.shape, jnp.float32) for table in tables],
            pltpu.SemaphoreType.DMA((3, tiles)),
            pltpu.SemaphoreType.DMA((9,)),
        ],
        compiler_params=pltpu.CompilerParams(vmem_limit_bytes=VMEM_LIMIT),
        name="prepare",
    )(*operands)


def finish_body(hid, wk, wv, part, out):
    for side, w in enumerate((wk, wv)):
        product = jnp.dot(hid[...], w[...], preferred_element_type=jnp.float32)
        out[side] = (part[side] + product).astype(jnp.bfloat16)


def finish(hid, wk, wv, part):
    vmem = pl.BlockSpec(memory_space=pltpu.VMEM)
    return pl.pallas_call(
        finish_body,
        in_specs=[vmem] * 4,
        out_specs=vmem,
        out_shape=jax.ShapeDtypeStruct(part.shape, jnp.bfloat16),
        compiler_params=pltpu.CompilerParams(vmem_limit_bytes=VMEM_LIMIT),
        name="finish",
    )(hid, wk, wv, part)


def span_slot(cells, offset, fixed, order, count, needle, owners, rows):
    if fixed:
        slot = jnp.int32(offset)
    else:
        offset = jnp.where(lax.rem(lax.axis_index("head"), 2) == 0, -offset, offset)
        cell = lax.axis_index("cell")
        evens = (cells + 1) // 2
        ring_at = jnp.where(lax.rem(cell, 2) == 0, cell // 2, cells - (cell + 1) // 2)
        at = lax.rem(ring_at + offset + cells, cells)
        slot = find_slot(owners, jnp.where(at < evens, 2 * at, 2 * (cells - at) - 1))
    place = order[0, jnp.maximum(slot, 0)]
    before = (slot >= 0) & (slot < count[0]) & (place < order[0, needle[0]])
    reach = jnp.where(before, rows, jnp.where(slot == needle[0], 0, -rows))
    return place, reach


def load_span(kv, place, tables, k_rot, v_aug, at):
    rows = kv.shape[1]
    keys = slice(at * rows, (at + 1) * rows)
    cosine, sine = table_at(*tables, place)
    for k in range(k_rot.shape[0]):
        lanes = slice(k * HD, (k + 1) * HD)
        k_rot[k, keys] = rotate(kv[0, :, lanes], cosine, sine)
        v_aug[k, :HD, keys] = kv[1, :, lanes].T
        v_aug[k, HD:, keys] = jnp.ones((v_aug.shape[1] - HD, rows), jnp.bfloat16)


def write_out(out, acc):
    for h in range(acc.shape[0]):
        total = acc[h, HD : HD + 1]
        out[:, h * HD : (h + 1) * HD] = (acc[h, :HD] * (1.0 / total)).astype(jnp.bfloat16).T


def reach_mask(shape, reach):
    key = lax.broadcasted_iota(jnp.int32, shape, 0)
    row = lax.broadcasted_iota(jnp.int32, shape, 1)
    return key - row <= reach


def shifted_attention(spans, slots_of, q_t, tables, out, m, acc, k_rot, v_aug):
    q_heads, _, rows = q_t.shape
    m[...] = jnp.full_like(m, NEG)
    acc[...] = jnp.zeros_like(acc)
    for kv, (place, reach) in zip(spans, slots_of):

        @pl.when(reach >= 0)
        def _():
            load_span(kv, place, tables, k_rot, v_aug, 0)

            def body(h, carry):
                s = jnp.dot(
                    k_rot[h // GROUP, :rows], q_t[h], preferred_element_type=jnp.float32
                )
                s = jnp.where(reach_mask(s.shape, reach), s, -jnp.inf)
                m_old = m[h]
                m_new = jnp.maximum(m_old, jnp.max(s, axis=0, keepdims=True))
                m[h] = m_new
                p = jnp.exp2((s - m_new) * COEF).astype(jnp.bfloat16)
                pv = jnp.dot(v_aug[h // GROUP, :, :rows], p, preferred_element_type=jnp.float32)
                acc[h] = acc[h] * jnp.exp2((m_old - m_new) * COEF) + pv[: acc.shape[1]]
                return carry

            lax.fori_loop(0, q_heads, body, 0)

    write_out(out, acc)


def attend_body(cells, offsets, every, fixed, first, last, order, count, needle, owners, q_t, row_t, place_t, *rest):
    rest = list(rest)
    spans = [rest.pop(0) for _ in offsets]
    acc_in = None if first else rest.pop(0)
    if last:
        past = [rest.pop(0) for _ in every]
        out, acc, k_rot, v_aug, seen, p_a, p_b, m = rest
    else:
        acc, k_rot, v_aug, seen, p_a, p_b = rest
    p_buf = (p_a, p_b)
    q_heads, _, rows = q_t.shape
    tables = (row_t, place_t)
    where = functools.partial(
        span_slot, cells, fixed=fixed, order=order, count=count, needle=needle, owners=owners, rows=rows
    )
    for at, (offset, kv) in enumerate(zip(offsets, spans)):
        place, reach = where(offset)
        mask = reach_mask((rows, rows), reach)
        seen[at * rows : (at + 1) * rows] = jnp.where(mask, 1.0, 0.0).astype(jnp.bfloat16)
        load_span(kv, place, tables, k_rot, v_aug, at)

    def weights(group, at):
        for g in range(PIPE):
            h = PIPE * group + g
            s = jnp.dot(k_rot[h // GROUP], q_t[h], preferred_element_type=jnp.float32)
            p_buf[at][g] = jnp.exp2(s * COEF).astype(jnp.bfloat16) * seen[...]

    def mix(group, at):
        for g in range(PIPE):
            h = PIPE * group + g
            pv = jnp.dot(v_aug[h // GROUP], p_buf[at][g], preferred_element_type=jnp.float32)
            pv = pv[: acc.shape[1]]
            acc[h] = pv if first else acc_in[h] + pv

    groups = q_heads // PIPE
    weights(0, 0)

    def body(i, carry):
        weights(2 * i + 1, 1)
        mix(2 * i, 0)
        weights(2 * i + 2, 0)
        mix(2 * i + 1, 1)
        return carry

    lax.fori_loop(0, groups // 2 - 1, body, 0)
    weights(groups - 1, 1)
    mix(groups - 2, 0)
    mix(groups - 1, 1)

    if last:
        write_out(out, acc)
        total = acc[:, HD : HD + 1]
        sound = (total > SAFE_LOW) & (total < SAFE_HIGH)

        @pl.when(jnp.max(jnp.where(sound, 0.0, 1.0)) > 0.0)
        def _():
            places = [where(offset) for offset in list(every) + list(offsets)]
            shifted_attention(past + spans, places, q_t, tables, out, m, acc, k_rot, v_aug)


def attend(cells, offsets, scalars, q_t, tables, blocks, acc, past=None, fixed=False):
    q_heads, _, rows = q_t.shape
    kv_heads = q_heads // GROUP
    first, last = acc is None, past is not None
    every, past_blocks = past if last else ((), ())
    smem = pl.BlockSpec(memory_space=pltpu.SMEM)
    vmem = pl.BlockSpec(memory_space=pltpu.VMEM)
    acc_shape = (q_heads, HD + 8, rows)
    keys = len(blocks) * rows
    operands = [q_t, *tables, *blocks]
    if not first:
        operands.append(acc)
    operands += past_blocks
    scratch = [
        pltpu.VMEM((kv_heads, keys, HD), jnp.bfloat16),
        pltpu.VMEM((kv_heads, HD + 16, keys), jnp.bfloat16),
        pltpu.VMEM((keys, rows), jnp.bfloat16),
        *[pltpu.VMEM((PIPE, keys, rows), jnp.bfloat16)] * 2,
    ]
    if last:
        out_shape = jax.ShapeDtypeStruct((rows, q_heads * HD), jnp.bfloat16)
        scratch = [pltpu.VMEM(acc_shape, jnp.float32)] + scratch
        scratch.append(pltpu.VMEM((q_heads, 1, rows), jnp.float32))
    else:
        out_shape = jax.ShapeDtypeStruct(acc_shape, jnp.float32)
    return pl.pallas_call(
        functools.partial(attend_body, cells, tuple(offsets), tuple(every), fixed, first, last),
        in_specs=[smem] * 4 + [vmem] * len(operands),
        out_specs=vmem,
        out_shape=out_shape,
        scratch_shapes=scratch,
        compiler_params=pltpu.CompilerParams(vmem_limit_bytes=VMEM_LIMIT),
        name="attend",
    )(*scalars, *operands)


def layer(cells, heads, hidden, w_key, w_value, queries, span_order, span_count, needle, owners):
    rows = hidden.shape[0]
    slots = span_order.shape[1]
    row_np, place_np = rotary_tables(rows, slots)
    tables = (jnp.asarray(row_np), jnp.asarray(place_np))
    scalars = (span_order, span_count, needle, owners.T)

    other = lax.ppermute(hidden, "head", [((h + 1) % heads, h) for h in range(heads)])
    part, q_t, wk_next, wv_next, *scalars = prepare(
        heads, scalars, hidden, w_key, w_value, queries, tables
    )
    own = finish(other, wk_next, wv_next, part)

    if cells > RING_LIMIT:
        gathered = lax.all_gather(own, "cell", axis=0)
        acc, blocks = None, []
        for s in range(slots):
            at = owners.reshape(-1)[s]
            block = lax.dynamic_index_in_dim(gathered, at, 0, keepdims=False)
            past = (range(s), blocks) if s == slots - 1 else None
            acc = attend(cells, (s,), scalars, q_t, tables, [block], acc, past, fixed=True)
            blocks.append(block)
        return acc

    ring = list(range(0, cells, 2)) + list(range(1, cells, 2))[::-1]

    def send(x, way):
        pairs = []
        for i in range(cells):
            for h in range(heads):
                to = ring[(i + (way if h % 2 == 0 else -way)) % cells]
                pairs.append((ring[i] * heads + h, to * heads + h))
        return lax.ppermute(x, ("cell", "head"), pairs)

    arrived = {0: own}
    for step in range(1, cells // 2 + 1):
        arrived[step] = send(arrived[step - 1], 1)
        if 2 * step < cells:
            arrived[-step] = send(arrived[1 - step], -1)

    acc, past = None, []
    plan = groups_of(cells)
    for i, offsets in enumerate(plan):
        blocks = [arrived[k] for k in offsets]
        final = (past, [arrived[k] for k in past]) if i == len(plan) - 1 else None
        acc = attend(cells, offsets, scalars, q_t, tables, blocks, acc, final)
        past = past + list(offsets)
    return acc


def groups_of(cells):
    order = [k for step in range(1, cells // 2 + 1) for k in (step, -step) if k > 0 or 2 * step < cells]
    return [(0,), (order[0],)] + [tuple(order[i : i + 2]) for i in range(1, len(order), 2)]


def solution(mesh):
    cells, heads = mesh.shape["cell"], mesh.shape["head"]
    in_specs = (
        P(("sweep", "cell"), "head"),
        P(None, "head"),
        P(None, "head"),
        P(("sweep", "cell"), "head"),
        P(("sweep", "cell"), None),
        P(("sweep", "cell")),
        P(("sweep", "cell")),
        P("sweep", None),
    )
    return jax.shard_map(
        functools.partial(layer, cells, heads),
        mesh=mesh,
        in_specs=in_specs,
        out_specs=P(("sweep", "cell"), "head"),
        check_vma=False,
    )
```
